32 devices in a mesh: tm: 16 (over z, y, x), ffn: 2 (over core).
Axes of the slice: x: 2, y: 2, z: 4, core: 2. Of those that a mesh axis runs over, the one named last changes fastest.
Arguments:
- frames: bfloat16 [32768, 512], P('tm'), may hold values from -60 to 60
- upstream: bfloat16 [32768, 512], P('tm'), may hold values from -6 to 6
- recording: int32 [32768], replicated, may hold values from 0 to 3, never falling along the last dimension, each value on 1 to 16384 neighbouring positions
- first_gain: float32 [512], replicated, may hold values from 0.1 to 1.9
- query_weight: bfloat16 [512, 512], P(None, 'ffn'), may hold values from -0.5 to 0.5
- key_weight: bfloat16 [512, 512], P(None, 'ffn'), may hold values from -0.5 to 0.5
- value_weight: bfloat16 [512, 512], P(None, 'ffn'), may hold values from -0.25 to 0.25
- out_weight: bfloat16 [512, 512], P('ffn'), may hold values from -0.25 to 0.25
- second_gain: float32 [512], replicated, may hold values from 0.1 to 1.9
- inner_weight: bfloat16 [512, 2048], P(None, 'ffn'), may hold values from -0.25 to 0.25
- outer_weight: bfloat16 [2048, 512], P('ffn'), may hold values from -0.125 to 0.125
Outputs:
- grad_frames: float32 [32768, 512], P(('tm', 'ffn'))
- grad_query_weight: float32 [512, 512], P(None, 'ffn')
- grad_key_weight: float32 [512, 512], P(None, 'ffn')
- grad_value_weight: float32 [512, 512], P(None, 'ffn')
- grad_out_weight: float32 [512, 512], P('ffn')
- grad_inner_weight: float32 [512, 2048], P(None, 'ffn')
- grad_outer_weight: float32 [2048, 512], P('ffn')
The draws below stay inside these ranges and needn't reach their ends.
Inputs may be any that keep to these rules, and one draw needn't show every extreme that they name: Ids never fall along time; each recording spans 1 to 16384 frames and one spans exactly that many.
All inputs are finite; a program needn't handle non-finite values.
Results may differ from the reference program's by a relative error of at most 0.025.
Values may be sent and summed in bfloat16 or wider, within the bound.
A program may use at most 128 MiB of HBM per device.

```python
import math
import jax
import jax.numpy as jnp
import numpy as np
from jax import lax

D = 512
HEADS = 8
FF = 2048
HEAD_DIM = 64
HALF = 256
FRAMES_DEV = 2048
TOKENS = 32768
RECORDINGS = 4
HEAD_GROUPS = 2


def projection_draw(key, salt):
    base = jax.random.truncated_normal(jax.random.fold_in(key, salt), -6.0, 6.0, (D, D), jnp.float32) / math.sqrt(D)
    return jnp.clip(base, -0.5, 0.5).astype(jnp.bfloat16)


def draw_query_weight(key, part):
    return projection_draw(key, 11)


def draw_key_weight(key, part):
    return projection_draw(key, 12)


def draw_frames(key, part):
    drawn = jax.random.truncated_normal(jax.random.fold_in(key, 13), -6.0, 6.0, (TOKENS, D), jnp.float32)
    return drawn.astype(jnp.bfloat16)


def shard_levels(key, shape, shards, low, largest):
    loudness, own = 1.0, jax.random.fold_in(key, 6)
    for dim, shards_of in shards:
        draws = jnp.exp(jax.random.uniform(jax.random.fold_in(own, dim), (shards_of,), jnp.float32, low / len(shards), largest / len(shards)))
        loudness = loudness * jnp.repeat(draws, shape[dim] // shards_of).reshape([-1 if axis == dim else 1 for axis in range(len(shape))])
    return loudness


def profile(count, total, reach, slope):
    portions = [(1 << 20) // math.isqrt(standing ** slope) + 1 for standing in range(2, count + 1)]
    spare, holding = total - reach - (count - 1), [1] * (count - 1)
    while spare > 0:
        candidates = [i for i in range(count - 1) if holding[i] < reach]
        mass, remaining = sum([portions[i] for i in candidates]), spare
        for i in candidates:
            more = min(reach - holding[i], max(1, remaining * portions[i] // mass), spare)
            holding[i] = holding[i] + more
            spare = spare - more
    return np.array([reach] + holding)


def ragged(key, amount, total, reach, skew):
    if amount == 2:
        one = jax.random.randint(key, (), max(1, total - reach), min(reach, total - 1) + 1)
        return jnp.stack([one, total - one])
    lengths = jnp.asarray(profile(amount, total, reach, skew), jnp.int32)
    couples = (amount - 1) // 2
    source_of, taker = lengths[1:1 + 2 * couples:2], lengths[2:2 + 2 * couples:2]
    margin = jnp.minimum(source_of - 1, reach - taker)
    passed = jax.random.randint(jax.random.fold_in(key, 1), (couples,), 0, 1 << 20) % (margin + 1)
    lengths = lengths.at[1:1 + 2 * couples:2].set(source_of - passed).at[2:2 + 2 * couples:2].set(taker + passed)
    return lengths[jax.random.permutation(jax.random.fold_in(key, 2), amount)]


def gaussian(own_key, shape, deviation, most, cuts=(), held_as=jnp.bfloat16):
    factor_of = shard_levels(own_key, shape, cuts, -0.22, 0.18) if cuts else 1.0
    entries = jax.random.normal(own_key, shape, jnp.float32) * deviation * factor_of
    return jnp.minimum(jnp.maximum(entries, -most), most).astype(held_as)


def setup_inputs(seed: int = 0) -> dict:
    keys = jax.random.split(jax.random.key(seed), 12)
    return {
        "frames": draw_frames(jax.random.fold_in(keys[11], 71), 0),
        "upstream": gaussian(keys[1], (TOKENS, D), 1.0, 6.0, ((0, 16),)),
        "recording": jnp.searchsorted(jnp.cumsum(ragged(keys[2], RECORDINGS, TOKENS, 8 * FRAMES_DEV, 0)), jnp.arange(TOKENS), side="right").astype(jnp.int32),
        "first_gain": jnp.clip(1.0 + 0.18 * jax.random.normal(keys[3], (D,), jnp.float32), 0.1, 1.9),
        "query_weight": draw_query_weight(jax.random.fold_in(keys[11], 71), 0),
        "key_weight": draw_key_weight(jax.random.fold_in(keys[11], 71), 0),
        "value_weight": gaussian(keys[6], (D, D), D ** -0.5, 0.25, ((1, 2),)),
        "out_weight": gaussian(keys[7], (D, D), D ** -0.5, 0.25, ((0, 2),)),
        "second_gain": jnp.clip(1.0 + 0.18 * jax.random.normal(keys[8], (D,), jnp.float32), 0.1, 1.9),
        "inner_weight": gaussian(keys[9], (D, FF), D ** -0.5, 0.25, ((1, 2),)),
        "outer_weight": gaussian(keys[10], (FF, D), FF ** -0.5, 0.125, ((0, 2),)),
    }


epsilon = 1e-05
masked_score = -1e+30

def layer_norm(inputs):
    center = lax.optimization_barrier(jnp.mean(inputs, axis=-1, keepdims=True))
    shifted = inputs - center
    inverse = lax.rsqrt(lax.optimization_barrier(jnp.mean(shifted * shifted, axis=-1, keepdims=True)) + epsilon)
    return (shifted * inverse, inverse)

def norm_back(grad_normed, scaled, inverse, gain):
    weighted = grad_normed * gain
    first_mean = lax.optimization_barrier(jnp.mean(weighted, axis=-1, keepdims=True))
    second_mean = lax.optimization_barrier(jnp.mean(weighted * scaled, axis=-1, keepdims=True))
    return inverse * (weighted - first_mean - scaled * second_mean)

def round_trip(array):
    return lax.optimization_barrier(array.astype(jnp.bfloat16)).astype(jnp.float32)

def grouped_sum(pairs):
    total = None
    for left, right in pairs:
        left_groups = left.astype(jnp.float32).reshape(left.shape[0], HEAD_GROUPS, left.shape[1] // HEAD_GROUPS)
        right_groups = right.astype(jnp.float32).reshape(HEAD_GROUPS, right.shape[0] // HEAD_GROUPS, right.shape[1])
        term = jnp.einsum('rgc,gco->gro', left_groups, right_groups)
        total = term if total is None else total + term
    rounded = round_trip(total)
    return lax.optimization_barrier(jnp.sum(rounded, axis=0))

def split_heads(block):
    return block.astype(jnp.float32).reshape(block.shape[0], HEADS, HEAD_DIM)

def block_allowed(record_query, record_key):
    block_rows = record_query.shape[0]
    offsets = lax.broadcasted_iota(jnp.int32, (block_rows, 2 * block_rows), 1) - lax.broadcasted_iota(jnp.int32, (block_rows, 2 * block_rows), 0)
    band = (offsets >= 0) & (offsets < block_rows)
    return band & (record_query[:, None] == record_key[None, :])

def softmax_block(query_block, key_block, allowed):
    scores = jnp.einsum('qhd,khd->hqk', query_block, key_block) * HEAD_DIM ** (-0.5)
    scores = jnp.where(allowed[None], scores, masked_score)
    peak = lax.optimization_barrier(jnp.max(scores, axis=-1, keepdims=True))
    weights = jnp.exp(scores - peak)
    return weights / lax.optimization_barrier(jnp.sum(weights, axis=-1, keepdims=True))

def block_pieces(block_index, queries, key_pad, value_pad, recording, record_pad):
    block_rows = 2 * HALF
    start = (block_index * block_rows).astype(jnp.int32)
    query_block = split_heads(lax.dynamic_slice_in_dim(queries, start, block_rows, 0))
    key_block = split_heads(lax.dynamic_slice_in_dim(key_pad, start, 2 * block_rows, 0))
    value_block = split_heads(lax.dynamic_slice_in_dim(value_pad, start, 2 * block_rows, 0))
    record_query = lax.dynamic_slice_in_dim(recording, start, block_rows, 0)
    record_key = lax.dynamic_slice_in_dim(record_pad, start, 2 * block_rows, 0)
    return (start, query_block, key_block, value_block, block_allowed(record_query, record_key))

def padded_inputs(key_rows, value_rows, recording):
    key_pad = jnp.pad(key_rows, ((HALF, HALF), (0, 0)))
    value_pad = jnp.pad(value_rows, ((HALF, HALF), (0, 0)))
    record_pad = jnp.pad(recording, (HALF, HALF), constant_values=-1)
    return (key_pad, value_pad, record_pad)

def attention_context(queries, key_rows, value_rows, recording):
    key_pad, value_pad, record_pad = padded_inputs(key_rows, value_rows, recording)
    block_rows = 2 * HALF

    def one_block(block_index):
        start, query_block, key_block, value_block, allowed = block_pieces(block_index, queries, key_pad, value_pad, recording, record_pad)
        probability_low = round_trip(softmax_block(query_block, key_block, allowed))
        context = jnp.einsum('hqk,khd->qhd', probability_low, value_block)
        return context.reshape(block_rows, D).astype(jnp.bfloat16)
    blocks = TOKENS // block_rows
    return lax.map(one_block, jnp.arange(blocks, dtype=jnp.int32)).reshape(TOKENS, D)

def intersection_add(pieces):
    block_rows = 2 * HALF
    lower = pieces[:, :block_rows]
    upper = pieces[:, block_rows:]
    padded = jnp.pad(lower, ((0, 1), (0, 0), (0, 0))) + jnp.pad(upper, ((1, 0), (0, 0), (0, 0)))
    return padded.reshape(-1, D)[HALF:HALF + TOKENS]

def attention_grads(queries, key_rows, value_rows, recording, grad_context):
    key_pad, value_pad, record_pad = padded_inputs(key_rows, value_rows, recording)
    block_rows = 2 * HALF

    def one_block(block_index):
        start, query_block, key_block, value_block, allowed = block_pieces(block_index, queries, key_pad, value_pad, recording, record_pad)
        grad_block = split_heads(lax.dynamic_slice_in_dim(grad_context, start, block_rows, 0))
        probability = softmax_block(query_block, key_block, allowed)
        probability_low = round_trip(probability)
        grad_prob = jnp.einsum('qhd,khd->hqk', grad_block, value_block)
        inner_sum = lax.optimization_barrier(jnp.sum(grad_prob * probability, axis=-1, keepdims=True))
        grad_scores = round_trip(probability * (grad_prob - inner_sum) * HEAD_DIM ** (-0.5))
        grad_query = jnp.einsum('hqk,khd->qhd', grad_scores, key_block).reshape(block_rows, D)
        grad_key = jnp.einsum('hqk,qhd->khd', grad_scores, query_block).reshape(2 * block_rows, D)
        grad_value = jnp.einsum('hqk,qhd->khd', probability_low, grad_block).reshape(2 * block_rows, D)
        return (grad_query, grad_key, grad_value)
    blocks = TOKENS // block_rows
    query_parts, key_parts, value_parts = lax.map(one_block, jnp.arange(blocks, dtype=jnp.int32))
    return (query_parts.reshape(TOKENS, D), intersection_add(key_parts), intersection_add(value_parts))

def reference(frames, upstream, recording, first_gain, query_weight, key_weight, value_weight, out_weight, second_gain, inner_weight, outer_weight):
    frames_wide = frames.astype(jnp.float32)
    upstream_wide = upstream.astype(jnp.float32)
    scaled_first, inverse_first = layer_norm(frames_wide)
    normed_first = (scaled_first * first_gain).astype(jnp.bfloat16)
    queries = jnp.dot(normed_first, query_weight, preferred_element_type=jnp.float32).astype(jnp.bfloat16)
    key_rows = jnp.dot(normed_first, key_weight, preferred_element_type=jnp.float32).astype(jnp.bfloat16)
    value_rows = jnp.dot(normed_first, value_weight, preferred_element_type=jnp.float32).astype(jnp.bfloat16)
    context = attention_context(queries, key_rows, value_rows, recording)
    middle = frames_wide + grouped_sum([(context, out_weight)])
    scaled_second, inverse_second = layer_norm(middle)
    normed_second = (scaled_second * second_gain).astype(jnp.bfloat16)
    inner_pre = jnp.dot(normed_second, inner_weight, preferred_element_type=jnp.float32)
    activation = jax.nn.silu(inner_pre).astype(jnp.bfloat16)
    sigmoid_inner = jax.nn.sigmoid(inner_pre)
    grad_act = jnp.dot(upstream, outer_weight.T, preferred_element_type=jnp.float32) * 0.5
    grad_inner = (grad_act * sigmoid_inner * (1.0 + inner_pre * (1.0 - sigmoid_inner))).astype(jnp.bfloat16)
    grad_second = grouped_sum([(grad_inner, inner_weight.T)])
    grad_middle = upstream_wide + norm_back(grad_second, scaled_second, inverse_second, second_gain)
    grad_middle_low = grad_middle.astype(jnp.bfloat16)
    grad_context = jnp.dot(grad_middle_low, out_weight.T, preferred_element_type=jnp.float32).astype(jnp.bfloat16)
    grad_query, grad_key, grad_value = attention_grads(queries, key_rows, value_rows, recording, grad_context)
    grad_query = grad_query.astype(jnp.bfloat16)
    grad_key = grad_key.astype(jnp.bfloat16)
    grad_value = grad_value.astype(jnp.bfloat16)
    grad_first = grouped_sum([(grad_query, query_weight.T), (grad_key, key_weight.T), (grad_value, value_weight.T)])
    grad_frames = grad_middle + norm_back(grad_first, scaled_first, inverse_first, first_gain)
    weight_scale = 1.0 / math.sqrt(TOKENS)
    grad_query_weight = jnp.dot(normed_first.T, grad_query, preferred_element_type=jnp.float32) * weight_scale
    grad_key_weight = jnp.dot(normed_first.T, grad_key, preferred_element_type=jnp.float32) * weight_scale
    grad_value_weight = jnp.dot(normed_first.T, grad_value, preferred_element_type=jnp.float32) * weight_scale
    grad_out_weight = jnp.dot(context.T, grad_middle_low, preferred_element_type=jnp.float32) * weight_scale
    grad_inner_weight = jnp.dot(normed_second.T, grad_inner, preferred_element_type=jnp.float32) * weight_scale
    grad_outer_weight = jnp.dot(activation.T, upstream, preferred_element_type=jnp.float32) * 0.5 * weight_scale
    return (grad_frames, grad_query_weight, grad_key_weight, grad_value_weight, grad_out_weight, grad_inner_weight, grad_outer_weight)
```

```python
import math

import jax
import jax.numpy as jnp
from jax import lax
from jax.experimental import pallas as pl
from jax.experimental.pallas import tpu as pltpu
from jax.sharding import PartitionSpec as P

HEAD_DIM = 64
HALF = 256


epsilon = 1e-05
masked_score = -1e30


def with_halo(cells, sides, width):
    for axis, dim in sides:
        count = lax.axis_size(axis)
        ends = count - 1
        head = lax.slice_in_dim(cells, 0, width, axis=dim)
        tail = lax.slice_in_dim(cells, cells.shape[dim] - width, cells.shape[dim], axis=dim)
        cells = jnp.concatenate(
            [
                lax.ppermute(tail, axis, [(i, (i + 1) % count) for i in range(ends)]),
                cells,
                lax.ppermute(head, axis, [((i + 1) % count, i) for i in range(ends)]),
            ],
            axis=dim,
        )
    return cells


def layer_norm(inputs):
    center = jnp.mean(inputs, axis=-1, keepdims=True)
    shifted = inputs - center
    inverse = lax.rsqrt(jnp.mean(shifted * shifted, axis=-1, keepdims=True) + epsilon)
    return (shifted * inverse, inverse)


def norm_back(grad_normed, scaled, inverse, gain):
    weighted = grad_normed * gain
    first_mean = jnp.mean(weighted, axis=-1, keepdims=True)
    second_mean = jnp.mean(weighted * scaled, axis=-1, keepdims=True)
    return inverse * (weighted - first_mean - scaled * second_mean)


def project(normed, weight):
    return jnp.dot(normed, weight, preferred_element_type=jnp.float32).astype(jnp.bfloat16)


def contract(left, right, dims):
    return lax.dot_general(left, right, (dims, ((), ())), preferred_element_type=jnp.float32)


def window_bias(record_query_ref, record_key_ref, start, rows, window):
    key_ids = record_key_ref[pl.ds(start, window), :]
    query_ids = record_query_ref[...]
    offsets = lax.broadcasted_iota(jnp.int32, (window, rows), 0) - lax.broadcasted_iota(
        jnp.int32, (window, rows), 1
    )
    allowed = (offsets >= 0) & (offsets < 2 * HALF) & (key_ids == query_ids)
    return jnp.where(allowed, 0.0, masked_score)


def head_mask(head, value):
    lanes = lax.broadcasted_iota(jnp.int32, (1, 2 * HEAD_DIM), 1)
    own = (lanes >= head * HEAD_DIM) & (lanes < (head + 1) * HEAD_DIM)
    return jnp.where(own, value, 0.0).astype(jnp.bfloat16)


def forward_kernel(query_ref, pair_ref, record_query_ref, record_key_ref, context_ref, lse_ref):
    rows, cols = query_ref.shape
    window = rows + 2 * HALF
    start = pl.multiple_of(pl.program_id(0) * rows, rows)
    bias = window_bias(record_query_ref, record_key_ref, start, rows, window)
    width = 2 * HEAD_DIM
    for pair in range(cols // width):
        lanes = slice(pair * width, (pair + 1) * width)
        key_tile = pair_ref[pl.ds(start, window), lanes]
        value_t = pair_ref[pl.ds(start, window), cols + pair * width : cols + (pair + 1) * width].T
        query_tile = query_ref[:, lanes]
        parts = []
        for head in range(2):
            query_head = query_tile * head_mask(head, HEAD_DIM ** (-0.5))
            scores = contract(key_tile, query_head, ((1,), (1,))) + bias
            peak = jnp.max(scores, axis=0, keepdims=True)
            weights = jnp.exp(scores - peak)
            total = jnp.sum(weights, axis=0, keepdims=True)
            mixed = contract(
                value_t[head * HEAD_DIM : (head + 1) * HEAD_DIM],
                weights.astype(jnp.bfloat16),
                ((1,), (0,)),
            )
            parts.append(mixed * (1.0 / total))
            lse_ref[2 * pair + head : 2 * pair + head + 1, :] = peak + jnp.log(total)
        context_ref[:, lanes] = jnp.concatenate(parts, axis=0).T.astype(jnp.bfloat16)


def backward_kernel(
    query_ref,
    pair_ref,
    grad_ref,
    lse_ref,
    record_query_ref,
    record_key_ref,
    grad_query_ref,
    own_ref,
    own_rim_ref,
    sent_rim_ref,
    total_ref,
):
    rows, cols = query_ref.shape
    window = rows + 2 * HALF
    step = pl.program_id(0)
    start = pl.multiple_of(step * rows, rows)
    width = 2 * HEAD_DIM

    @pl.when(step == 0)
    def _():
        total_ref[...] = jnp.zeros_like(total_ref)

    bias = window_bias(record_query_ref, record_key_ref, start, rows, window)
    for pair in range(cols // width):
        lanes = slice(pair * width, (pair + 1) * width)
        value_lanes = slice(cols + pair * width, cols + (pair + 1) * width)
        key_tile = pair_ref[pl.ds(start, window), lanes]
        value_tile = pair_ref[pl.ds(start, window), value_lanes]
        key_t = key_tile.T
        parts = []
        grad_key = None
        for head in range(2):
            query_head = query_ref[:, lanes] * head_mask(head, HEAD_DIM ** (-0.5))
            grad_head = grad_ref[:, lanes] * head_mask(head, 1.0)
            scores = contract(key_tile, query_head, ((1,), (1,))) + bias
            index = 2 * pair + head
            probability = jnp.exp(scores - lse_ref[index : index + 1, :])
            grad_prob = contract(value_tile, grad_head, ((1,), (1,)))
            inner = jnp.sum(probability * grad_prob, axis=0, keepdims=True)
            grad_scores = (probability * (grad_prob - inner)).astype(jnp.bfloat16)
            value_term = contract(probability.astype(jnp.bfloat16), grad_head, ((1,), (0,)))
            key_term = contract(grad_scores, query_head, ((1,), (0,)))
            grad_key = key_term if grad_key is None else grad_key + key_term
            grad_value = value_term if head == 0 else grad_value + value_term
            parts.append(
                contract(
                    key_t[head * HEAD_DIM : (head + 1) * HEAD_DIM], grad_scores, ((1,), (0,))
                )
            )
        grad_query = jnp.concatenate(parts, axis=0).T * HEAD_DIM ** (-0.5)
        grad_query_ref[:, lanes] = grad_query.astype(jnp.bfloat16)
        total_ref[pl.ds(start, window), lanes] += grad_key
        total_ref[pl.ds(start, window), value_lanes] += grad_value

    @pl.when(step == pl.num_programs(0) - 1)
    def _():
        slab = own_ref.shape[0]
        own_ref[...] = total_ref[HALF : HALF + slab, :].astype(jnp.bfloat16)
        own_rim_ref[:HALF] = total_ref[HALF : 2 * HALF, :]
        own_rim_ref[HALF:] = total_ref[slab : slab + HALF, :]
        sent_rim_ref[:HALF] = total_ref[:HALF, :].astype(jnp.bfloat16)
        sent_rim_ref[HALF:] = total_ref[slab + HALF :, :].astype(jnp.bfloat16)


def whole(shape):
    return pl.BlockSpec(shape, lambda i: (0, 0))


def attention_forward(queries, pairs, record_query, record_key):
    slab, cols = queries.shape
    heads = cols // HEAD_DIM
    rows = HALF
    return pl.pallas_call(
        forward_kernel,
        grid=(slab // rows,),
        in_specs=[
            pl.BlockSpec((rows, cols), lambda i: (i, 0)),
            whole(pairs.shape),
            pl.BlockSpec((1, rows), lambda i: (0, i)),
            whole(record_key.shape),
        ],
        out_specs=[
            pl.BlockSpec((rows, cols), lambda i: (i, 0)),
            pl.BlockSpec((heads, rows), lambda i: (0, i)),
        ],
        out_shape=[
            jax.ShapeDtypeStruct((slab, cols), jnp.bfloat16),
            jax.ShapeDtypeStruct((heads, slab), jnp.float32),
        ],
        cost_estimate=pl.CostEstimate(
            flops=4 * slab * 3 * HALF * cols * 4,
            bytes_accessed=slab * cols * 8,
            transcendentals=slab * 3 * HALF * heads,
        ),
        name="attention_forward",
    )(queries, pairs, record_query, record_key)


def attention_backward(queries, pairs, grad_context, lse, record_query, record_key):
    slab, cols = queries.shape
    heads = cols // HEAD_DIM
    rows = HALF
    return pl.pallas_call(
        backward_kernel,
        grid=(slab // rows,),
        in_specs=[
            pl.BlockSpec((rows, cols), lambda i: (i, 0)),
            whole(pairs.shape),
            pl.BlockSpec((rows, cols), lambda i: (i, 0)),
            pl.BlockSpec((heads, rows), lambda i: (0, i)),
            pl.BlockSpec((1, rows), lambda i: (0, i)),
            whole(record_key.shape),
        ],
        out_specs=[
            pl.BlockSpec((rows, cols), lambda i: (i, 0)),
            whole((slab, 2 * cols)),
            whole((2 * HALF, 2 * cols)),
            whole((2 * HALF, 2 * cols)),
        ],
        out_shape=[
            jax.ShapeDtypeStruct((slab, cols), jnp.bfloat16),
            jax.ShapeDtypeStruct((slab, 2 * cols), jnp.bfloat16),
            jax.ShapeDtypeStruct((2 * HALF, 2 * cols), jnp.float32),
            jax.ShapeDtypeStruct((2 * HALF, 2 * cols), jnp.bfloat16),
        ],
        scratch_shapes=[pltpu.VMEM(pairs.shape, jnp.float32)],
        cost_estimate=pl.CostEstimate(
            flops=10 * slab * 3 * HALF * cols * 4,
            bytes_accessed=slab * cols * 16,
            transcendentals=slab * 3 * HALF * heads,
        ),
        name="attention_backward",
    )(queries, pairs, grad_context, lse, record_query, record_key)


def shift(array, axis, by):
    count = lax.axis_size(axis)
    return lax.ppermute(array, axis, [(i, (i + by) % count) for i in range(count)])


def group_sum(term):
    low = term.astype(jnp.bfloat16)
    total = low.astype(jnp.float32)
    for by in range(1, lax.axis_size("ffn")):
        total = total + shift(low, "ffn", by).astype(jnp.float32)
    return total


def group_scatter(term):
    low = term.astype(jnp.bfloat16)
    count = lax.axis_size("ffn")
    rows = low.shape[0] // count
    me = lax.axis_index("ffn")
    total = lax.dynamic_slice_in_dim(low, me * rows, rows, 0).astype(jnp.float32)
    for by in range(1, count):
        piece = lax.dynamic_slice_in_dim(low, ((me + by) % count) * rows, rows, 0)
        total = total + shift(piece, "ffn", by).astype(jnp.float32)
    return total


def local(
    frames,
    upstream,
    recording,
    first_gain,
    query_weight,
    key_weight,
    value_weight,
    out_weight,
    second_gain,
    inner_weight,
    outer_weight,
):
    slab_rows = frames.shape[0]
    head_cols = query_weight.shape[1]
    share_rows = slab_rows // lax.axis_size("ffn")
    share_start = lax.axis_index("ffn") * share_rows
    record_pad = jnp.pad(recording, (HALF, HALF), constant_values=-1)
    record_ext = lax.dynamic_slice_in_dim(
        record_pad, lax.axis_index("tm") * slab_rows, slab_rows + 2 * HALF
    )
    frames_wide = frames.astype(jnp.float32)
    upstream_wide = upstream.astype(jnp.float32)
    scaled_first, inverse_first = layer_norm(frames_wide)
    normed_first = (scaled_first * first_gain).astype(jnp.bfloat16)
    queries = project(normed_first, query_weight)
    key_rows = project(normed_first, key_weight)
    value_rows = project(normed_first, value_weight)
    key_value = jnp.concatenate([key_rows, value_rows], axis=1)
    key_value_ext = with_halo(key_value, (("tm", 0),), HALF)
    record_query = record_ext[HALF : HALF + slab_rows].reshape(1, slab_rows)
    record_key = record_ext.reshape(slab_rows + 2 * HALF, 1)
    context, lse = attention_forward(queries, key_value_ext, record_query, record_key)
    partial_value = jnp.dot(context, out_weight, preferred_element_type=jnp.float32)
    middle = frames_wide + group_sum(partial_value)
    scaled_second, inverse_second = layer_norm(middle)
    normed_second = (scaled_second * second_gain).astype(jnp.bfloat16)
    inner_pre = jnp.dot(normed_second, inner_weight, preferred_element_type=jnp.float32)
    activation = jax.nn.silu(inner_pre).astype(jnp.bfloat16)
    sigmoid_inner = jax.nn.sigmoid(inner_pre)
    grad_act = jnp.dot(upstream, outer_weight.T, preferred_element_type=jnp.float32) * 0.5
    grad_inner = (grad_act * sigmoid_inner * (1.0 + inner_pre * (1.0 - sigmoid_inner))).astype(
        jnp.bfloat16
    )
    grad_outer_terms = jnp.dot(activation.T, upstream, preferred_element_type=jnp.float32) * 0.5
    grad_inner_terms = jnp.dot(normed_second.T, grad_inner, preferred_element_type=jnp.float32)
    grad_second_part = jnp.dot(grad_inner, inner_weight.T, preferred_element_type=jnp.float32)
    grad_second = group_sum(grad_second_part)
    grad_middle = upstream_wide + norm_back(grad_second, scaled_second, inverse_second, second_gain)
    grad_middle_low = grad_middle.astype(jnp.bfloat16)
    grad_middle_share = lax.dynamic_slice_in_dim(grad_middle, share_start, share_rows, 0)
    grad_out_terms = jnp.dot(context.T, grad_middle_low, preferred_element_type=jnp.float32)
    grad_context = jnp.dot(
        grad_middle_low, out_weight.T, preferred_element_type=jnp.float32
    ).astype(jnp.bfloat16)
    grad_query_low, own, own_rim, sent_rim = attention_backward(
        queries, key_value_ext, grad_context, lse, record_query, record_key
    )
    count = lax.axis_size("tm")
    from_lower = lax.ppermute(sent_rim[HALF:], "tm", [(i, i + 1) for i in range(count - 1)])
    from_upper = lax.ppermute(sent_rim[:HALF], "tm", [(i + 1, i) for i in range(count - 1)])
    grad_pairs = jnp.concatenate(
        [
            (own_rim[:HALF] + from_lower.astype(jnp.float32)).astype(jnp.bfloat16),
            own[HALF : slab_rows - HALF],
            (own_rim[HALF:] + from_upper.astype(jnp.float32)).astype(jnp.bfloat16),
        ],
        axis=0,
    )
    grad_key_low = grad_pairs[:, :head_cols]
    grad_value_low = grad_pairs[:, head_cols:]
    grad_query_terms = jnp.dot(normed_first.T, grad_query_low, preferred_element_type=jnp.float32)
    grad_key_terms = jnp.dot(normed_first.T, grad_key_low, preferred_element_type=jnp.float32)
    grad_value_terms = jnp.dot(normed_first.T, grad_value_low, preferred_element_type=jnp.float32)
    grad_first_part = jnp.dot(grad_query_low, query_weight.T, preferred_element_type=jnp.float32)
    grad_first_part = grad_first_part + jnp.dot(
        grad_key_low, key_weight.T, preferred_element_type=jnp.float32
    )
    grad_first_part = grad_first_part + jnp.dot(
        grad_value_low, value_weight.T, preferred_element_type=jnp.float32
    )
    grad_first_share = group_scatter(grad_first_part)
    scaled_share = lax.dynamic_slice_in_dim(scaled_first, share_start, share_rows, 0)
    inverse_share = lax.dynamic_slice_in_dim(inverse_first, share_start, share_rows, 0)
    grad_frames = grad_middle_share + norm_back(
        grad_first_share, scaled_share, inverse_share, first_gain
    )
    weight_scale = 1.0 / math.sqrt(recording.shape[0])
    first_totals = lax.psum(
        (grad_inner_terms.astype(jnp.bfloat16), grad_outer_terms.astype(jnp.bfloat16)), "tm"
    )
    attention_terms = tuple(
        term.astype(jnp.bfloat16)
        for term in (grad_query_terms, grad_key_terms, grad_value_terms, grad_out_terms)
    )
    attention_terms, first_totals = lax.optimization_barrier((attention_terms, first_totals))
    totals = tuple(
        total.astype(jnp.float32) for total in lax.psum(attention_terms, "tm") + first_totals
    )
    return (grad_frames,) + tuple((total * weight_scale for total in totals))


def solution(mesh):
    in_specs = (
        P("tm", None),
        P("tm", None),
        P(),
        P(),
        P(None, "ffn"),
        P(None, "ffn"),
        P(None, "ffn"),
        P("ffn", None),
        P(),
        P(None, "ffn"),
        P("ffn", None),
    )
    out_specs = (
        P(("tm", "ffn"), None),
        P(None, "ffn"),
        P(None, "ffn"),
        P(None, "ffn"),
        P("ffn", None),
        P(None, "ffn"),
        P("ffn", None),
    )
    return jax.shard_map(local, mesh=mesh, in_specs=in_specs, out_specs=out_specs, check_vma=False)
```

```python
import functools
import math

import jax
import jax.numpy as jnp
from jax import lax
from jax.experimental import pallas as pl
from jax.experimental.pallas import tpu as pltpu
from jax.sharding import PartitionSpec as P

HEAD_DIM = 64
HALF = 256


epsilon = 1e-05
masked_score = -1e30


def with_halo(cells, sides, width):
    for axis, dim in sides:
        count = lax.axis_size(axis)
        ends = count - 1
        head = lax.slice_in_dim(cells, 0, width, axis=dim)
        tail = lax.slice_in_dim(cells, cells.shape[dim] - width, cells.shape[dim], axis=dim)
        cells = jnp.concatenate(
            [
                lax.ppermute(tail, axis, [(i, (i + 1) % count) for i in range(ends)]),
                cells,
                lax.ppermute(head, axis, [((i + 1) % count, i) for i in range(ends)]),
            ],
            axis=dim,
        )
    return cells


def layer_norm(inputs):
    center = jnp.mean(inputs, axis=-1, keepdims=True)
    shifted = inputs - center
    inverse = lax.rsqrt(jnp.mean(shifted * shifted, axis=-1, keepdims=True) + epsilon)
    return (shifted * inverse, inverse)


def norm_back(grad_normed, scaled, inverse, gain):
    weighted = grad_normed * gain
    first_mean = jnp.mean(weighted, axis=-1, keepdims=True)
    second_mean = jnp.mean(weighted * scaled, axis=-1, keepdims=True)
    return inverse * (weighted - first_mean - scaled * second_mean)


def project(normed, weight):
    return jnp.dot(normed, weight, preferred_element_type=jnp.float32).astype(jnp.bfloat16)


def contract(left, right, dims):
    return lax.dot_general(left, right, (dims, ((), ())), preferred_element_type=jnp.float32)


def window_bias(record_query_ref, record_key_ref, start, rows, window):
    key_ids = record_key_ref[pl.ds(start, window), :]
    query_ids = record_query_ref[...]
    offsets = lax.broadcasted_iota(jnp.int32, (window, rows), 0) - lax.broadcasted_iota(
        jnp.int32, (window, rows), 1
    )
    allowed = (offsets >= 0) & (offsets < 2 * HALF) & (key_ids == query_ids)
    return jnp.where(allowed, 0.0, masked_score)


def head_mask(head, value):
    lanes = lax.broadcasted_iota(jnp.int32, (1, 2 * HEAD_DIM), 1)
    own = (lanes >= head * HEAD_DIM) & (lanes < (head + 1) * HEAD_DIM)
    return jnp.where(own, value, 0.0).astype(jnp.bfloat16)


def forward_kernel(query_ref, pair_ref, record_query_ref, record_key_ref, context_ref, lse_ref):
    rows, cols = query_ref.shape
    window = rows + 2 * HALF
    start = pl.multiple_of(pl.program_id(0) * rows, rows)
    bias = window_bias(record_query_ref, record_key_ref, start, rows, window)
    width = 2 * HEAD_DIM
    for pair in range(cols // width):
        lanes = slice(pair * width, (pair + 1) * width)
        key_tile = pair_ref[pl.ds(start, window), lanes]
        value_t = pair_ref[pl.ds(start, window), cols + pair * width : cols + (pair + 1) * width].T
        query_tile = query_ref[:, lanes]
        parts = []
        for head in range(2):
            query_head = query_tile * head_mask(head, HEAD_DIM ** (-0.5))
            scores = contract(key_tile, query_head, ((1,), (1,))) + bias
            peak = jnp.max(scores, axis=0, keepdims=True)
            weights = jnp.exp(scores - peak)
            total = jnp.sum(weights, axis=0, keepdims=True)
            mixed = contract(
                value_t[head * HEAD_DIM : (head + 1) * HEAD_DIM],
                weights.astype(jnp.bfloat16),
                ((1,), (0,)),
            )
            parts.append(mixed * (1.0 / total))
            lse_ref[2 * pair + head : 2 * pair + head + 1, :] = peak + jnp.log(total)
        context_ref[:, lanes] = jnp.concatenate(parts, axis=0).T.astype(jnp.bfloat16)


def backward_kernel(
    query_ref,
    pair_ref,
    grad_ref,
    lse_ref,
    record_query_ref,
    record_key_ref,
    grad_query_ref,
    own_ref,
    own_rim_ref,
    sent_rim_ref,
    total_ref,
):
    rows, cols = query_ref.shape
    window = rows + 2 * HALF
    step = pl.program_id(0)
    start = pl.multiple_of(step * rows, rows)
    width = 2 * HEAD_DIM

    @pl.when(step == 0)
    def _():
        total_ref[...] = jnp.zeros_like(total_ref)

    bias = window_bias(record_query_ref, record_key_ref, start, rows, window)
    for pair in range(cols // width):
        lanes = slice(pair * width, (pair + 1) * width)
        value_lanes = slice(cols + pair * width, cols + (pair + 1) * width)
        key_tile = pair_ref[pl.ds(start, window), lanes]
        value_tile = pair_ref[pl.ds(start, window), value_lanes]
        key_t = key_tile.T
        parts = []
        grad_key = None
        for head in range(2):
            query_head = query_ref[:, lanes] * head_mask(head, HEAD_DIM ** (-0.5))
            grad_head = grad_ref[:, lanes] * head_mask(head, 1.0)
            scores = contract(key_tile, query_head, ((1,), (1,))) + bias
            index = 2 * pair + head
            probability = jnp.exp(scores - lse_ref[index : index + 1, :])
            grad_prob = contract(value_tile, grad_head, ((1,), (1,)))
            inner = jnp.sum(probability * grad_prob, axis=0, keepdims=True)
            grad_scores = (probability * (grad_prob - inner)).astype(jnp.bfloat16)
            value_term = contract(probability.astype(jnp.bfloat16), grad_head, ((1,), (0,)))
            key_term = contract(grad_scores, query_head, ((1,), (0,)))
            grad_key = key_term if grad_key is None else grad_key + key_term
            grad_value = value_term if head == 0 else grad_value + value_term
            parts.append(
                contract(
                    key_t[head * HEAD_DIM : (head + 1) * HEAD_DIM], grad_scores, ((1,), (0,))
                )
            )
        grad_query = jnp.concatenate(parts, axis=0).T * HEAD_DIM ** (-0.5)
        grad_query_ref[:, lanes] = grad_query.astype(jnp.bfloat16)
        total_ref[pl.ds(start, window), lanes] += grad_key
        total_ref[pl.ds(start, window), value_lanes] += grad_value

    @pl.when(step == pl.num_programs(0) - 1)
    def _():
        slab = own_ref.shape[0]
        own_ref[...] = total_ref[HALF : HALF + slab, :].astype(jnp.bfloat16)
        own_rim_ref[:HALF] = total_ref[HALF : 2 * HALF, :]
        own_rim_ref[HALF:] = total_ref[slab : slab + HALF, :]
        sent_rim_ref[:HALF] = total_ref[:HALF, :].astype(jnp.bfloat16)
        sent_rim_ref[HALF:] = total_ref[slab + HALF :, :].astype(jnp.bfloat16)


def whole(shape):
    return pl.BlockSpec(shape, lambda i: (0, 0))


def attention_forward(queries, pairs, record_query, record_key):
    slab, cols = queries.shape
    heads = cols // HEAD_DIM
    rows = HALF
    return pl.pallas_call(
        forward_kernel,
        grid=(slab // rows,),
        in_specs=[
            pl.BlockSpec((rows, cols), lambda i: (i, 0)),
            whole(pairs.shape),
            pl.BlockSpec((1, rows), lambda i: (0, i)),
            whole(record_key.shape),
        ],
        out_specs=[
            pl.BlockSpec((rows, cols), lambda i: (i, 0)),
            pl.BlockSpec((heads, rows), lambda i: (0, i)),
        ],
        out_shape=[
            jax.ShapeDtypeStruct((slab, cols), jnp.bfloat16),
            jax.ShapeDtypeStruct((heads, slab), jnp.float32),
        ],
        cost_estimate=pl.CostEstimate(
            flops=4 * slab * 3 * HALF * cols * 4,
            bytes_accessed=slab * cols * 8,
            transcendentals=slab * 3 * HALF * heads,
        ),
        name="attention_forward",
    )(queries, pairs, record_query, record_key)


def attention_backward(queries, pairs, grad_context, lse, record_query, record_key):
    slab, cols = queries.shape
    heads = cols // HEAD_DIM
    rows = HALF
    return pl.pallas_call(
        backward_kernel,
        grid=(slab // rows,),
        in_specs=[
            pl.BlockSpec((rows, cols), lambda i: (i, 0)),
            whole(pairs.shape),
            pl.BlockSpec((rows, cols), lambda i: (i, 0)),
            pl.BlockSpec((heads, rows), lambda i: (0, i)),
            pl.BlockSpec((1, rows), lambda i: (0, i)),
            whole(record_key.shape),
        ],
        out_specs=[
            pl.BlockSpec((rows, cols), lambda i: (i, 0)),
            whole((slab, 2 * cols)),
            whole((2 * HALF, 2 * cols)),
            whole((2 * HALF, 2 * cols)),
        ],
        out_shape=[
            jax.ShapeDtypeStruct((slab, cols), jnp.bfloat16),
            jax.ShapeDtypeStruct((slab, 2 * cols), jnp.bfloat16),
            jax.ShapeDtypeStruct((2 * HALF, 2 * cols), jnp.float32),
            jax.ShapeDtypeStruct((2 * HALF, 2 * cols), jnp.bfloat16),
        ],
        scratch_shapes=[pltpu.VMEM(pairs.shape, jnp.float32)],
        cost_estimate=pl.CostEstimate(
            flops=10 * slab * 3 * HALF * cols * 4,
            bytes_accessed=slab * cols * 16,
            transcendentals=slab * 3 * HALF * heads,
        ),
        name="attention_backward",
    )(queries, pairs, grad_context, lse, record_query, record_key)


def shift(array, axis, by):
    count = lax.axis_size(axis)
    return lax.ppermute(array, axis, [(i, (i + by) % count) for i in range(count)])


def group_sum(term):
    low = term.astype(jnp.bfloat16)
    total = low.astype(jnp.float32)
    for by in range(1, lax.axis_size("ffn")):
        total = total + shift(low, "ffn", by).astype(jnp.float32)
    return total


def group_scatter(term):
    low = term.astype(jnp.bfloat16)
    count = lax.axis_size("ffn")
    rows = low.shape[0] // count
    me = lax.axis_index("ffn")
    total = lax.dynamic_slice_in_dim(low, me * rows, rows, 0).astype(jnp.float32)
    for by in range(1, count):
        piece = lax.dynamic_slice_in_dim(low, ((me + by) % count) * rows, rows, 0)
        total = total + shift(piece, "ffn", by).astype(jnp.float32)
    return total


def sum_kernel(
    inner, scale, x_ref, out_ref, near, mid, far, gathered, near_sems, far_sems, back_sems, last_sems
):
    me = lax.axis_index("tm")
    outer = x_ref.shape[1]
    row = lax.div(me, inner)
    col = lax.rem(me, inner)
    near_peers = [row * inner + lax.rem(col + k, inner) for k in range(1, inner)]
    far_peers = [lax.rem(row + k, outer) * inner + col for k in range(1, outer)]
    barrier = pltpu.get_barrier_semaphore()
    for peer in near_peers + far_peers:
        pl.semaphore_signal(
            barrier, inc=1, device_id={"tm": peer}, device_id_type=pl.DeviceIdType.MESH
        )
    pl.semaphore_wait(barrier, inner + outer - 2)

    def send(source, target, sems, slot, peer):
        copy = pltpu.make_async_remote_copy(
            src_ref=source,
            dst_ref=target,
            send_sem=sems.at[0, slot],
            recv_sem=sems.at[1, slot],
            device_id={"tm": peer},
            device_id_type=pl.DeviceIdType.MESH,
        )
        copy.start()
        return copy

    copies = [
        send(x_ref.at[lax.rem(col + k, inner)], near.at[k - 1], near_sems, k - 1, near_peers[k - 1])
        for k in range(1, inner)
    ]
    for copy in copies:
        copy.wait()
    total = x_ref[col].astype(jnp.float32)
    for k in range(inner - 1):
        total = total + near[k].astype(jnp.float32)
    mid[...] = total.astype(jnp.bfloat16)
    copies = [
        send(mid.at[lax.rem(row + k, outer)], far.at[k - 1], far_sems, k - 1, far_peers[k - 1])
        for k in range(1, outer)
    ]
    for copy in copies:
        copy.wait()
    total = mid[row].astype(jnp.float32)
    for k in range(outer - 1):
        total = total + far[k].astype(jnp.float32)
    gathered[col, row] = total.astype(jnp.bfloat16)
    copies = [
        send(gathered.at[col, row], gathered.at[col, row], back_sems, k, far_peers[k])
        for k in range(outer - 1)
    ]
    for copy in copies:
        copy.wait()
    copies = [
        send(gathered.at[col], gathered.at[col], last_sems, k, near_peers[k])
        for k in range(inner - 1)
    ]
    for copy in copies:
        copy.wait()
    out_ref[...] = gathered[...].astype(jnp.float32) * scale


def slab_sum(stacked, scale):
    count = lax.axis_size("tm")
    inner = max(d for d in range(1, count + 1) if count % d == 0 and d * d <= count)
    outer = count // inner
    rows, cols = stacked.shape
    piece = rows // count
    low = jnp.bfloat16
    total = pl.pallas_call(
        functools.partial(sum_kernel, inner, scale),
        out_shape=jax.ShapeDtypeStruct((inner, outer, piece, cols), jnp.float32),
        in_specs=[pl.BlockSpec(memory_space=pltpu.VMEM)],
        out_specs=pl.BlockSpec(memory_space=pltpu.VMEM),
        scratch_shapes=[
            pltpu.VMEM((inner - 1, outer, piece, cols), low),
            pltpu.VMEM((outer, piece, cols), low),
            pltpu.VMEM((outer - 1, piece, cols), low),
            pltpu.VMEM((inner, outer, piece, cols), low),
            pltpu.SemaphoreType.DMA((2, inner - 1)),
            pltpu.SemaphoreType.DMA((2, outer - 1)),
            pltpu.SemaphoreType.DMA((2, outer - 1)),
            pltpu.SemaphoreType.DMA((2, inner - 1)),
        ],
        compiler_params=pltpu.CompilerParams(collective_id=0, has_side_effects=True),
        cost_estimate=pl.CostEstimate(
            flops=rows * cols * 4, bytes_accessed=rows * cols * 100, transcendentals=0
        ),
        name="slab_sum",
    )(stacked.reshape(inner, outer, piece, cols))
    return total.reshape(rows, cols)


def local(
    frames,
    upstream,
    recording,
    first_gain,
    query_weight,
    key_weight,
    value_weight,
    out_weight,
    second_gain,
    inner_weight,
    outer_weight,
):
    slab_rows = frames.shape[0]
    head_cols = query_weight.shape[1]
    share_rows = slab_rows // lax.axis_size("ffn")
    share_start = lax.axis_index("ffn") * share_rows
    record_pad = jnp.pad(recording, (HALF, HALF), constant_values=-1)
    record_ext = lax.dynamic_slice_in_dim(
        record_pad, lax.axis_index("tm") * slab_rows, slab_rows + 2 * HALF
    )
    frames_wide = frames.astype(jnp.float32)
    upstream_wide = upstream.astype(jnp.float32)
    scaled_first, inverse_first = layer_norm(frames_wide)
    normed_first = (scaled_first * first_gain).astype(jnp.bfloat16)
    queries = project(normed_first, query_weight)
    key_rows = project(normed_first, key_weight)
    value_rows = project(normed_first, value_weight)
    key_value = jnp.concatenate([key_rows, value_rows], axis=1)
    key_value_ext = with_halo(key_value, (("tm", 0),), HALF)
    record_query = record_ext[HALF : HALF + slab_rows].reshape(1, slab_rows)
    record_key = record_ext.reshape(slab_rows + 2 * HALF, 1)
    context, lse = attention_forward(queries, key_value_ext, record_query, record_key)
    partial_value = jnp.dot(context, out_weight, preferred_element_type=jnp.float32)
    middle = frames_wide + group_sum(partial_value)
    scaled_second, inverse_second = layer_norm(middle)
    normed_second = (scaled_second * second_gain).astype(jnp.bfloat16)
    inner_pre = jnp.dot(normed_second, inner_weight, preferred_element_type=jnp.float32)
    activation = jax.nn.silu(inner_pre).astype(jnp.bfloat16)
    sigmoid_inner = jax.nn.sigmoid(inner_pre)
    grad_act = jnp.dot(upstream, outer_weight.T, preferred_element_type=jnp.float32) * 0.5
    grad_inner = (grad_act * sigmoid_inner * (1.0 + inner_pre * (1.0 - sigmoid_inner))).astype(
        jnp.bfloat16
    )
    grad_outer_terms = jnp.dot(activation.T, upstream, preferred_element_type=jnp.float32) * 0.5
    grad_inner_terms = jnp.dot(normed_second.T, grad_inner, preferred_element_type=jnp.float32)
    grad_second_part = jnp.dot(grad_inner, inner_weight.T, preferred_element_type=jnp.float32)
    grad_second = group_sum(grad_second_part)
    grad_middle = upstream_wide + norm_back(grad_second, scaled_second, inverse_second, second_gain)
    grad_middle_low = grad_middle.astype(jnp.bfloat16)
    grad_middle_share = lax.dynamic_slice_in_dim(grad_middle, share_start, share_rows, 0)
    grad_out_terms = jnp.dot(context.T, grad_middle_low, preferred_element_type=jnp.float32)
    grad_context = jnp.dot(
        grad_middle_low, out_weight.T, preferred_element_type=jnp.float32
    ).astype(jnp.bfloat16)
    grad_query_low, own, own_rim, sent_rim = attention_backward(
        queries, key_value_ext, grad_context, lse, record_query, record_key
    )
    count = lax.axis_size("tm")
    from_lower = lax.ppermute(sent_rim[HALF:], "tm", [(i, i + 1) for i in range(count - 1)])
    from_upper = lax.ppermute(sent_rim[:HALF], "tm", [(i + 1, i) for i in range(count - 1)])
    grad_pairs = jnp.concatenate(
        [
            (own_rim[:HALF] + from_lower.astype(jnp.float32)).astype(jnp.bfloat16),
            own[HALF : slab_rows - HALF],
            (own_rim[HALF:] + from_upper.astype(jnp.float32)).astype(jnp.bfloat16),
        ],
        axis=0,
    )
    grad_key_low = grad_pairs[:, :head_cols]
    grad_value_low = grad_pairs[:, head_cols:]
    grad_query_terms = jnp.dot(normed_first.T, grad_query_low, preferred_element_type=jnp.float32)
    grad_key_terms = jnp.dot(normed_first.T, grad_key_low, preferred_element_type=jnp.float32)
    grad_value_terms = jnp.dot(normed_first.T, grad_value_low, preferred_element_type=jnp.float32)
    grad_first_part = jnp.dot(grad_query_low, query_weight.T, preferred_element_type=jnp.float32)
    grad_first_part = grad_first_part + jnp.dot(
        grad_key_low, key_weight.T, preferred_element_type=jnp.float32
    )
    grad_first_part = grad_first_part + jnp.dot(
        grad_value_low, value_weight.T, preferred_element_type=jnp.float32
    )
    grad_first_share = group_scatter(grad_first_part)
    scaled_share = lax.dynamic_slice_in_dim(scaled_first, share_start, share_rows, 0)
    inverse_share = lax.dynamic_slice_in_dim(inverse_first, share_start, share_rows, 0)
    grad_frames = grad_middle_share + norm_back(
        grad_first_share, scaled_share, inverse_share, first_gain
    )
    weight_scale = 1.0 / math.sqrt(recording.shape[0])
    first_totals = lax.psum(
        (grad_inner_terms.astype(jnp.bfloat16), grad_outer_terms.astype(jnp.bfloat16)), "tm"
    )
    blocks = grad_out_terms.shape[1] // head_cols
    stacked = jnp.concatenate(
        [grad_query_terms, grad_key_terms, grad_value_terms]
        + [grad_out_terms[:, i * head_cols : (i + 1) * head_cols] for i in range(blocks)],
        axis=0,
    ).astype(jnp.bfloat16)
    summed = slab_sum(stacked, weight_scale)
    depth = grad_query_terms.shape[0]
    out_rows = grad_out_terms.shape[0]
    grad_out = jnp.concatenate(
        [summed[3 * depth + i * out_rows : 3 * depth + (i + 1) * out_rows] for i in range(blocks)],
        axis=1,
    )
    first_totals, grad_out = lax.optimization_barrier((first_totals, grad_out))
    return (
        grad_frames,
        summed[:depth],
        summed[depth : 2 * depth],
        summed[2 * depth : 3 * depth],
        grad_out,
    ) + tuple(total.astype(jnp.float32) * weight_scale for total in first_totals)


def solution(mesh):
    in_specs = (
        P("tm", None),
        P("tm", None),
        P(),
        P(),
        P(None, "ffn"),
        P(None, "ffn"),
        P(None, "ffn"),
        P("ffn", None),
        P(),
        P(None, "ffn"),
        P("ffn", None),
    )
    out_specs = (
        P(("tm", "ffn"), None),
        P(None, "ffn"),
        P(None, "ffn"),
        P(None, "ffn"),
        P("ffn", None),
        P(None, "ffn"),
        P("ffn", None),
    )
    return jax.shard_map(local, mesh=mesh, in_specs=in_specs, out_specs=out_specs, check_vma=False)
```

```python
import functools
import math

import jax
import jax.numpy as jnp
from jax import lax
from jax.experimental import pallas as pl
from jax.experimental.pallas import tpu as pltpu
from jax.sharding import PartitionSpec as P

HEAD_DIM = 64
HALF = 256


epsilon = 1e-05
masked_score = -1e30


def with_halo(cells, sides, width):
    for axis, dim in sides:
        count = lax.axis_size(axis)
        ends = count - 1
        head = lax.slice_in_dim(cells, 0, width, axis=dim)
        tail = lax.slice_in_dim(cells, cells.shape[dim] - width, cells.shape[dim], axis=dim)
        cells = jnp.concatenate(
            [
                lax.ppermute(tail, axis, [(i, (i + 1) % count) for i in range(ends)]),
                cells,
                lax.ppermute(head, axis, [((i + 1) % count, i) for i in range(ends)]),
            ],
            axis=dim,
        )
    return cells


def layer_norm(inputs):
    center = jnp.mean(inputs, axis=-1, keepdims=True)
    shifted = inputs - center
    inverse = lax.rsqrt(jnp.mean(shifted * shifted, axis=-1, keepdims=True) + epsilon)
    return (shifted * inverse, inverse)


def norm_back(grad_normed, scaled, inverse, gain):
    weighted = grad_normed * gain
    first_mean = jnp.mean(weighted, axis=-1, keepdims=True)
    second_mean = jnp.mean(weighted * scaled, axis=-1, keepdims=True)
    return inverse * (weighted - first_mean - scaled * second_mean)


def project(normed, weight):
    return jnp.dot(normed, weight, preferred_element_type=jnp.float32).astype(jnp.bfloat16)


def contract(left, right, dims):
    return lax.dot_general(left, right, (dims, ((), ())), preferred_element_type=jnp.float32)


def window_bias(record_query_ref, record_key_ref, start, rows, window):
    key_ids = record_key_ref[pl.ds(start, window), :]
    query_ids = record_query_ref[...]
    offsets = lax.broadcasted_iota(jnp.int32, (window, rows), 0) - lax.broadcasted_iota(
        jnp.int32, (window, rows), 1
    )
    allowed = (offsets >= 0) & (offsets < 2 * HALF) & (key_ids == query_ids)
    return jnp.where(allowed, 0.0, masked_score)


def head_mask(head, value):
    lanes = lax.broadcasted_iota(jnp.int32, (1, 2 * HEAD_DIM), 1)
    own = (lanes >= head * HEAD_DIM) & (lanes < (head + 1) * HEAD_DIM)
    return jnp.where(own, value, 0.0).astype(jnp.bfloat16)


def forward_kernel(
    query_ref, pair_ref, record_query_ref, record_key_ref, weight_ref, context_ref, lse_ref, term_ref
):
    rows, cols = query_ref.shape
    window = rows + 2 * HALF
    start = pl.multiple_of(pl.program_id(0) * rows, rows)
    bias = window_bias(record_query_ref, record_key_ref, start, rows, window)
    width = 2 * HEAD_DIM
    for pair in range(cols // width):
        lanes = slice(pair * width, (pair + 1) * width)
        key_tile = pair_ref[pl.ds(start, window), lanes]
        value_t = pair_ref[pl.ds(start, window), cols + pair * width : cols + (pair + 1) * width].T
        query_tile = query_ref[:, lanes]
        parts = []
        for head in range(2):
            query_head = query_tile * head_mask(head, HEAD_DIM ** (-0.5))
            scores = contract(key_tile, query_head, ((1,), (1,))) + bias
            peak = jnp.max(scores, axis=0, keepdims=True)
            weights = jnp.exp(scores - peak)
            total = jnp.sum(weights, axis=0, keepdims=True)
            mixed = contract(
                value_t[head * HEAD_DIM : (head + 1) * HEAD_DIM],
                weights.astype(jnp.bfloat16),
                ((1,), (0,)),
            )
            parts.append(mixed * (1.0 / total))
            lse_ref[2 * pair + head : 2 * pair + head + 1, :] = peak + jnp.log(total)
        context_ref[:, lanes] = jnp.concatenate(parts, axis=0).T.astype(jnp.bfloat16)
    term_ref[...] = contract(context_ref[...], weight_ref[...], ((1,), (0,))).astype(jnp.bfloat16)


def backward_kernel(
    query_ref,
    pair_ref,
    grad_ref,
    lse_ref,
    record_query_ref,
    record_key_ref,
    grad_query_ref,
    own_ref,
    own_rim_ref,
    sent_rim_ref,
    total_ref,
):
    rows, cols = query_ref.shape
    window = rows + 2 * HALF
    step = pl.program_id(0)
    start = pl.multiple_of(step * rows, rows)
    width = 2 * HEAD_DIM

    @pl.when(step == 0)
    def _():
        total_ref[...] = jnp.zeros_like(total_ref)

    bias = window_bias(record_query_ref, record_key_ref, start, rows, window)
    for pair in range(cols // width):
        lanes = slice(pair * width, (pair + 1) * width)
        value_lanes = slice(cols + pair * width, cols + (pair + 1) * width)
        key_tile = pair_ref[pl.ds(start, window), lanes]
        value_tile = pair_ref[pl.ds(start, window), value_lanes]
        key_t = key_tile.T
        parts = []
        grad_key = None
        for head in range(2):
            query_head = query_ref[:, lanes] * head_mask(head, HEAD_DIM ** (-0.5))
            grad_head = grad_ref[:, lanes] * head_mask(head, 1.0)
            scores = contract(key_tile, query_head, ((1,), (1,))) + bias
            index = 2 * pair + head
            probability = jnp.exp(scores - lse_ref[index : index + 1, :])
            grad_prob = contract(value_tile, grad_head, ((1,), (1,)))
            inner = jnp.sum(probability * grad_prob, axis=0, keepdims=True)
            grad_scores = (probability * (grad_prob - inner)).astype(jnp.bfloat16)
            value_term = contract(probability.astype(jnp.bfloat16), grad_head, ((1,), (0,)))
            key_term = contract(grad_scores, query_head, ((1,), (0,)))
            grad_key = key_term if grad_key is None else grad_key + key_term
            grad_value = value_term if head == 0 else grad_value + value_term
            parts.append(
                contract(
                    key_t[head * HEAD_DIM : (head + 1) * HEAD_DIM], grad_scores, ((1,), (0,))
                )
            )
        grad_query = jnp.concatenate(parts, axis=0).T * HEAD_DIM ** (-0.5)
        grad_query_ref[:, lanes] = grad_query.astype(jnp.bfloat16)
        total_ref[pl.ds(start, window), lanes] += grad_key
        total_ref[pl.ds(start, window), value_lanes] += grad_value

    @pl.when(step == pl.num_programs(0) - 1)
    def _():
        slab = own_ref.shape[0]
        own_ref[...] = total_ref[HALF : HALF + slab, :].astype(jnp.bfloat16)
        own_rim_ref[:HALF] = total_ref[HALF : 2 * HALF, :]
        own_rim_ref[HALF:] = total_ref[slab : slab + HALF, :]
        sent_rim_ref[:HALF] = total_ref[:HALF, :].astype(jnp.bfloat16)
        sent_rim_ref[HALF:] = total_ref[slab + HALF :, :].astype(jnp.bfloat16)


def whole(shape):
    return pl.BlockSpec(shape, lambda i: (0, 0))


def attention_forward(queries, pairs, record_query, record_key, weight):
    slab, cols = queries.shape
    heads = cols // HEAD_DIM
    rows = HALF
    return pl.pallas_call(
        forward_kernel,
        grid=(slab // rows,),
        in_specs=[
            pl.BlockSpec((rows, cols), lambda i: (i, 0)),
            whole(pairs.shape),
            pl.BlockSpec((1, rows), lambda i: (0, i)),
            whole(record_key.shape),
            whole(weight.shape),
        ],
        out_specs=[
            pl.BlockSpec((rows, cols), lambda i: (i, 0)),
            pl.BlockSpec((heads, rows), lambda i: (0, i)),
            pl.BlockSpec((rows, weight.shape[1]), lambda i: (i, 0)),
        ],
        out_shape=[
            jax.ShapeDtypeStruct((slab, cols), jnp.bfloat16),
            jax.ShapeDtypeStruct((heads, slab), jnp.float32),
            jax.ShapeDtypeStruct((slab, weight.shape[1]), jnp.bfloat16),
        ],
        cost_estimate=pl.CostEstimate(
            flops=4 * slab * 3 * HALF * cols * 4,
            bytes_accessed=slab * cols * 8,
            transcendentals=slab * 3 * HALF * heads,
        ),
        name="attention_forward",
    )(queries, pairs, record_query, record_key, weight)


def attention_backward(queries, pairs, grad_context, lse, record_query, record_key):
    slab, cols = queries.shape
    heads = cols // HEAD_DIM
    rows = HALF
    return pl.pallas_call(
        backward_kernel,
        grid=(slab // rows,),
        in_specs=[
            pl.BlockSpec((rows, cols), lambda i: (i, 0)),
            whole(pairs.shape),
            pl.BlockSpec((rows, cols), lambda i: (i, 0)),
            pl.BlockSpec((heads, rows), lambda i: (0, i)),
            pl.BlockSpec((1, rows), lambda i: (0, i)),
            whole(record_key.shape),
        ],
        out_specs=[
            pl.BlockSpec((rows, cols), lambda i: (i, 0)),
            whole((slab, 2 * cols)),
            whole((2 * HALF, 2 * cols)),
            whole((2 * HALF, 2 * cols)),
        ],
        out_shape=[
            jax.ShapeDtypeStruct((slab, cols), jnp.bfloat16),
            jax.ShapeDtypeStruct((slab, 2 * cols), jnp.bfloat16),
            jax.ShapeDtypeStruct((2 * HALF, 2 * cols), jnp.float32),
            jax.ShapeDtypeStruct((2 * HALF, 2 * cols), jnp.bfloat16),
        ],
        scratch_shapes=[pltpu.VMEM(pairs.shape, jnp.float32)],
        cost_estimate=pl.CostEstimate(
            flops=10 * slab * 3 * HALF * cols * 4,
            bytes_accessed=slab * cols * 16,
            transcendentals=slab * 3 * HALF * heads,
        ),
        name="attention_backward",
    )(queries, pairs, grad_context, lse, record_query, record_key)


def shift(array, axis, by):
    count = lax.axis_size(axis)
    return lax.ppermute(array, axis, [(i, (i + by) % count) for i in range(count)])


def group_sum(term):
    low = term.astype(jnp.bfloat16)
    total = low.astype(jnp.float32)
    for by in range(1, lax.axis_size("ffn")):
        total = total + shift(low, "ffn", by).astype(jnp.float32)
    return total


def group_scatter(term):
    low = term.astype(jnp.bfloat16)
    count = lax.axis_size("ffn")
    rows = low.shape[0] // count
    me = lax.axis_index("ffn")
    total = lax.dynamic_slice_in_dim(low, me * rows, rows, 0).astype(jnp.float32)
    for by in range(1, count):
        piece = lax.dynamic_slice_in_dim(low, ((me + by) % count) * rows, rows, 0)
        total = total + shift(piece, "ffn", by).astype(jnp.float32)
    return total


def sum_kernel(
    inner, scale, x_ref, out_ref, near, mid, far, gathered, near_sems, far_sems, back_sems, last_sems
):
    me = lax.axis_index("tm")
    outer = x_ref.shape[1]
    row = lax.div(me, inner)
    col = lax.rem(me, inner)
    near_peers = [row * inner + lax.rem(col + k, inner) for k in range(1, inner)]
    far_peers = [lax.rem(row + k, outer) * inner + col for k in range(1, outer)]
    barrier = pltpu.get_barrier_semaphore()
    for peer in near_peers + far_peers:
        pl.semaphore_signal(
            barrier, inc=1, device_id={"tm": peer}, device_id_type=pl.DeviceIdType.MESH
        )
    pl.semaphore_wait(barrier, inner + outer - 2)

    def send(source, target, sems, slot, peer):
        copy = pltpu.make_async_remote_copy(
            src_ref=source,
            dst_ref=target,
            send_sem=sems.at[0, slot],
            recv_sem=sems.at[1, slot],
            device_id={"tm": peer},
            device_id_type=pl.DeviceIdType.MESH,
        )
        copy.start()
        return copy

    copies = [
        send(x_ref.at[lax.rem(col + k, inner)], near.at[k - 1], near_sems, k - 1, near_peers[k - 1])
        for k in range(1, inner)
    ]
    for copy in copies:
        copy.wait()
    total = x_ref[col].astype(jnp.float32)
    for k in range(inner - 1):
        total = total + near[k].astype(jnp.float32)
    mid[...] = total.astype(jnp.bfloat16)
    copies = [
        send(mid.at[lax.rem(row + k, outer)], far.at[k - 1], far_sems, k - 1, far_peers[k - 1])
        for k in range(1, outer)
    ]
    for copy in copies:
        copy.wait()
    total = mid[row].astype(jnp.float32)
    for k in range(outer - 1):
        total = total + far[k].astype(jnp.float32)
    gathered[col, row] = total.astype(jnp.bfloat16)
    copies = [
        send(gathered.at[col, row], gathered.at[col, row], back_sems, k, far_peers[k])
        for k in range(outer - 1)
    ]
    for copy in copies:
        copy.wait()
    copies = [
        send(gathered.at[col], gathered.at[col], last_sems, k, near_peers[k])
        for k in range(inner - 1)
    ]
    for copy in copies:
        copy.wait()
    out_ref[...] = gathered[...].astype(jnp.float32) * scale


def slab_sum(stacked, scale):
    count = lax.axis_size("tm")
    inner = max(d for d in range(1, count + 1) if count % d == 0 and d * d <= count)
    outer = count // inner
    rows, cols = stacked.shape
    piece = rows // count
    low = jnp.bfloat16
    total = pl.pallas_call(
        functools.partial(sum_kernel, inner, scale),
        out_shape=jax.ShapeDtypeStruct((inner, outer, piece, cols), jnp.float32),
        in_specs=[pl.BlockSpec(memory_space=pltpu.VMEM)],
        out_specs=pl.BlockSpec(memory_space=pltpu.VMEM),
        scratch_shapes=[
            pltpu.VMEM((inner - 1, outer, piece, cols), low),
            pltpu.VMEM((outer, piece, cols), low),
            pltpu.VMEM((outer - 1, piece, cols), low),
            pltpu.VMEM((inner, outer, piece, cols), low),
            pltpu.SemaphoreType.DMA((2, inner - 1)),
            pltpu.SemaphoreType.DMA((2, outer - 1)),
            pltpu.SemaphoreType.DMA((2, outer - 1)),
            pltpu.SemaphoreType.DMA((2, inner - 1)),
        ],
        compiler_params=pltpu.CompilerParams(collective_id=0, has_side_effects=True),
        cost_estimate=pl.CostEstimate(
            flops=rows * cols * 4, bytes_accessed=rows * cols * 100, transcendentals=0
        ),
        name="slab_sum",
    )(stacked.reshape(inner, outer, piece, cols))
    return total.reshape(rows, cols)


def local(
    frames,
    upstream,
    recording,
    first_gain,
    query_weight,
    key_weight,
    value_weight,
    out_weight,
    second_gain,
    inner_weight,
    outer_weight,
):
    slab_rows = frames.shape[0]
    head_cols = query_weight.shape[1]
    share_rows = slab_rows // lax.axis_size("ffn")
    share_start = lax.axis_index("ffn") * share_rows
    record_pad = jnp.pad(recording, (HALF, HALF), constant_values=-1)
    record_ext = lax.dynamic_slice_in_dim(
        record_pad, lax.axis_index("tm") * slab_rows, slab_rows + 2 * HALF
    )
    frames_wide = frames.astype(jnp.float32)
    upstream_wide = upstream.astype(jnp.float32)
    scaled_first, inverse_first = layer_norm(frames_wide)
    normed_first = (scaled_first * first_gain).astype(jnp.bfloat16)
    queries = project(normed_first, query_weight)
    key_rows = project(normed_first, key_weight)
    value_rows = project(normed_first, value_weight)
    key_value = jnp.concatenate([key_rows, value_rows], axis=1)
    key_value_ext = with_halo(key_value, (("tm", 0),), HALF)
    record_query = record_ext[HALF : HALF + slab_rows].reshape(1, slab_rows)
    record_key = record_ext.reshape(slab_rows + 2 * HALF, 1)
    context, lse, partial_value = attention_forward(
        queries, key_value_ext, record_query, record_key, out_weight
    )
    middle = frames_wide + group_sum(partial_value)
    scaled_second, inverse_second = layer_norm(middle)
    normed_second = (scaled_second * second_gain).astype(jnp.bfloat16)
    inner_pre = jnp.dot(normed_second, inner_weight, preferred_element_type=jnp.float32)
    activation = jax.nn.silu(inner_pre).astype(jnp.bfloat16)
    sigmoid_inner = jax.nn.sigmoid(inner_pre)
    grad_act = jnp.dot(upstream, outer_weight.T, preferred_element_type=jnp.float32) * 0.5
    grad_inner = (grad_act * sigmoid_inner * (1.0 + inner_pre * (1.0 - sigmoid_inner))).astype(
        jnp.bfloat16
    )
    grad_outer_terms = jnp.dot(activation.T, upstream, preferred_element_type=jnp.float32) * 0.5
    grad_inner_terms = jnp.dot(normed_second.T, grad_inner, preferred_element_type=jnp.float32)
    grad_second_part = jnp.dot(grad_inner, inner_weight.T, preferred_element_type=jnp.float32)
    grad_second = group_sum(grad_second_part)
    grad_middle = upstream_wide + norm_back(grad_second, scaled_second, inverse_second, second_gain)
    grad_middle_low = grad_middle.astype(jnp.bfloat16)
    grad_middle_share = lax.dynamic_slice_in_dim(grad_middle, share_start, share_rows, 0)
    grad_out_terms = jnp.dot(context.T, grad_middle_low, preferred_element_type=jnp.float32)
    grad_context = jnp.dot(
        grad_middle_low, out_weight.T, preferred_element_type=jnp.float32
    ).astype(jnp.bfloat16)
    grad_query_low, own, own_rim, sent_rim = attention_backward(
        queries, key_value_ext, grad_context, lse, record_query, record_key
    )
    count = lax.axis_size("tm")
    from_lower = lax.ppermute(sent_rim[HALF:], "tm", [(i, i + 1) for i in range(count - 1)])
    from_upper = lax.ppermute(sent_rim[:HALF], "tm", [(i + 1, i) for i in range(count - 1)])
    grad_pairs = jnp.concatenate(
        [
            (own_rim[:HALF] + from_lower.astype(jnp.float32)).astype(jnp.bfloat16),
            own[HALF : slab_rows - HALF],
            (own_rim[HALF:] + from_upper.astype(jnp.float32)).astype(jnp.bfloat16),
        ],
        axis=0,
    )
    grad_key_low = grad_pairs[:, :head_cols]
    grad_value_low = grad_pairs[:, head_cols:]
    grad_query_terms = jnp.dot(normed_first.T, grad_query_low, preferred_element_type=jnp.float32)
    grad_key_terms = jnp.dot(normed_first.T, grad_key_low, preferred_element_type=jnp.float32)
    grad_value_terms = jnp.dot(normed_first.T, grad_value_low, preferred_element_type=jnp.float32)
    grad_first_part = jnp.dot(grad_query_low, query_weight.T, preferred_element_type=jnp.float32)
    grad_first_part = grad_first_part + jnp.dot(
        grad_key_low, key_weight.T, preferred_element_type=jnp.float32
    )
    grad_first_part = grad_first_part + jnp.dot(
        grad_value_low, value_weight.T, preferred_element_type=jnp.float32
    )
    grad_first_share = group_scatter(grad_first_part)
    scaled_share = lax.dynamic_slice_in_dim(scaled_first, share_start, share_rows, 0)
    inverse_share = lax.dynamic_slice_in_dim(inverse_first, share_start, share_rows, 0)
    grad_frames = grad_middle_share + norm_back(
        grad_first_share, scaled_share, inverse_share, first_gain
    )
    weight_scale = 1.0 / math.sqrt(recording.shape[0])
    first_totals = lax.psum(
        (grad_inner_terms.astype(jnp.bfloat16), grad_outer_terms.astype(jnp.bfloat16)), "tm"
    )
    blocks = grad_out_terms.shape[1] // head_cols
    stacked = jnp.concatenate(
        [grad_query_terms, grad_key_terms, grad_value_terms]
        + [grad_out_terms[:, i * head_cols : (i + 1) * head_cols] for i in range(blocks)],
        axis=0,
    ).astype(jnp.bfloat16)
    summed = slab_sum(stacked, weight_scale)
    depth = grad_query_terms.shape[0]
    out_rows = grad_out_terms.shape[0]
    grad_out = jnp.concatenate(
        [summed[3 * depth + i * out_rows : 3 * depth + (i + 1) * out_rows] for i in range(blocks)],
        axis=1,
    )
    first_totals, grad_out = lax.optimization_barrier((first_totals, grad_out))
    return (
        grad_frames,
        summed[:depth],
        summed[depth : 2 * depth],
        summed[2 * depth : 3 * depth],
        grad_out,
    ) + tuple(total.astype(jnp.float32) * weight_scale for total in first_totals)


def solution(mesh):
    in_specs = (
        P("tm", None),
        P("tm", None),
        P(),
        P(),
        P(None, "ffn"),
        P(None, "ffn"),
        P(None, "ffn"),
        P("ffn", None),
        P(),
        P(None, "ffn"),
        P("ffn", None),
    )
    out_specs = (
        P(("tm", "ffn"), None),
        P(None, "ffn"),
        P(None, "ffn"),
        P(None, "ffn"),
        P("ffn", None),
        P(None, "ffn"),
        P("ffn", None),
    )
    return jax.shard_map(local, mesh=mesh, in_specs=in_specs, out_specs=out_specs, check_vma=False)
```
